256 devices in a mesh: var: 2 (over z_lo), lat: 128 (over y, x, z_hi, core).
Axes of the slice: x: 4, y: 4, z: 8 (z_hi: 4, z_lo: 2; z = z_hi * 2 + z_lo), core: 2. Of those that a mesh axis runs over, the one named last changes fastest.
Arguments:
- grad_grid: bfloat16 [2, 768, 70, 1536], P('var', 'lat'), may hold values from -6 to 6
- remap: float32 [2, 70, 70], P('var'), may hold values from -0.75 to 0.75
- modes: float32 [2, 70, 70], P('var'), may hold values from -0.75 to 0.75
- balance: float32 [70, 70], replicated, may hold values from -0.75 to 0.75
- legendre: float32 [384, 768, 384], P('lat'), may hold values from -0.21875 to 0.21875
- control: float32 [2, 384, 140, 384], P('var', 'lat'), may hold values from -6 to 6
- step_size: float32 [2], P('var'), may hold values from 0.2 to 0.8
- owner_slots: int32 [384], replicated, may hold values from 0 to 383, each once
Outputs:
- updated: float32 [2, 384, 140, 384], P('var', 'lat')
- increment: bfloat16 [2, 768, 70, 1536], P('var', 'lat')
The draws below stay inside these ranges and needn't reach their ends.
Inputs may be any that keep to these rules, and one draw needn't show every extreme that they name: `owner_slots`: each zonal wavenumber below 384 stands in exactly one owner slot; lat index d holds slots d * 3 to (d + 1) * 3 - 1.
All inputs are finite; a program needn't handle non-finite values.
Results may differ from the reference program's by a relative error of at most 0.001.
Values sent between devices are 32-bit elements; how exact they have to be, the bound alone decides.
A program may use at most 64 MiB of HBM per device.

```python
import math
import jax
import jax.numpy as jnp
from jax import lax

NLON = 1536
NLAT = 768
LEV = 70
M = 384
NN = 384
N_LAT = 128


def levels(own_key, extent, split, least, top_value):
    level = 1.0
    for axis_at, shards_of in split:
        heights = jax.random.uniform(jax.random.fold_in(jax.random.fold_in(own_key, 6), axis_at), (shards_of,), jnp.float32, least / len(split), top_value / len(split))
        level = level * jnp.repeat(jnp.exp(heights), extent[axis_at] // shards_of).reshape((-1,) + (1,) * (len(extent) - 1 - axis_at))
    return level


def bell_draw(rng, extent, spread, most, split=(), kind=jnp.bfloat16):
    level = levels(rng, extent, split, -0.22, 0.18) if split else 1.0
    entries = jax.random.normal(rng, extent, jnp.float32) * spread * level
    return jnp.minimum(jnp.maximum(entries, -most), most).astype(kind)


def setup_inputs(seed: int = 0) -> dict:
    splits = jax.random.split(jax.random.key(seed), 9)
    return {
        "grad_grid": bell_draw(splits[0], (2, NLAT, LEV, NLON), 1.0, 6.0, ((0, 2), (1, 128))),
        "remap": bell_draw(splits[1], (2, LEV, LEV), LEV ** -0.5, 0.75, ((0, 2),), jnp.float32),
        "modes": bell_draw(splits[2], (2, LEV, LEV), LEV ** -0.5, 0.75, ((0, 2),), jnp.float32),
        "balance": bell_draw(splits[3], (LEV, LEV), LEV ** -0.5, 0.75, (), jnp.float32),
        "legendre": bell_draw(splits[4], (M, NLAT, NN), NLAT ** -0.5, 0.21875, ((0, 128),), jnp.float32),
        "control": bell_draw(splits[5], (2, M, 2 * LEV, NN), 1.0, 6.0, ((0, 2), (1, 128)), jnp.float32),
        "step_size": jnp.clip(0.2 + 0.6 * jax.random.uniform(splits[6], (2,), jnp.float32) ** levels(splits[6], (2,), ((0, 2),), -0.2, 0.2), 0.2, 0.8),
        "owner_slots": jax.random.permutation(splits[7], M).astype(jnp.int32),
    }


highest = lax.Precision.HIGHEST

def make_waves(owner_slots, lon_count):
    longitude = lax.iota(jnp.int32, lon_count)
    phases = longitude[:, None] * owner_slots[None, :].astype(jnp.int32) % lon_count
    angles = phases.astype(jnp.float32) * (2.0 * math.pi / lon_count)
    factor = math.sqrt(2.0 / lon_count)
    return jnp.stack([jnp.cos(angles), jnp.sin(angles)], axis=1) * factor

def reference(grad_grid, remap, modes, balance, legendre, control, step_size, owner_slots):
    wave_table = make_waves(owner_slots, NLON)
    lat_block = NLAT // N_LAT
    spectral_adj = []
    for variable in range(2):

        def grid_block(lat_piece, variable=variable):
            lifted = jnp.einsum('ik,lij->lkj', remap[variable], lat_piece.astype(jnp.float32), precision=highest)
            return jnp.einsum('lkj,jcs->slck', lifted, wave_table, precision=highest)
        pieces = lax.map(grid_block, grad_grid[variable].reshape(N_LAT, lat_block, LEV, NLON))
        fourier_adj = jnp.transpose(pieces, (1, 0, 2, 3, 4)).reshape(M, NLAT, 2 * LEV)
        coef = jnp.einsum('sln,slq->sqn', legendre, fourier_adj, precision=highest)
        spectral_adj.append(coef.reshape(M, 2, LEV, NN))
    carried = spectral_adj[0] + jnp.einsum('ik,scin->sckn', balance, spectral_adj[1], precision=highest)
    mode_psi = jnp.einsum('ik,scin->sckn', modes[0], carried, precision=highest)
    mode_mass = jnp.einsum('ik,scin->sckn', modes[1], spectral_adj[1], precision=highest)
    mode_adj = [mode_psi.reshape(M, 2 * LEV, NN), mode_mass.reshape(M, 2 * LEV, NN)]
    updated = [control[v] - step_size[v] * (control[v] + mode_adj[v]) for v in range(2)]
    coef_psi = jnp.einsum('ki,scin->sckn', modes[0], updated[0].reshape(M, 2, LEV, NN), precision=highest)
    coef_mass = jnp.einsum('ki,scin->sckn', modes[1], updated[1].reshape(M, 2, LEV, NN), precision=highest)
    coef_mass = coef_mass + jnp.einsum('ki,scin->sckn', balance, coef_psi, precision=highest)
    level_coef = [coef_psi, coef_mass]
    increments = []
    for variable in range(2):
        fourier = jnp.einsum('sln,sqn->slq', legendre, level_coef[variable].reshape(M, 2 * LEV, NN), precision=highest)
        blocks = jnp.transpose(fourier.reshape(M, N_LAT, lat_block, 2, LEV), (1, 0, 2, 3, 4))

        def wave_block(coef_piece, variable=variable):
            lowered = jnp.einsum('slck,jcs->lkj', coef_piece, wave_table, precision=highest)
            return jnp.einsum('ik,lkj->lij', remap[variable], lowered, precision=highest).astype(jnp.bfloat16)
        grid_out = lax.map(wave_block, blocks)
        increments.append(grid_out.reshape(NLAT, LEV, NLON))
    return (jnp.stack(updated), jnp.stack(increments))
```

```python
import functools
import math

import jax
import jax.numpy as jnp
from jax import lax
from jax.experimental import pallas as pl
from jax.experimental.pallas import tpu as pltpu
from jax.sharding import PartitionSpec as P

MESH = pl.DeviceIdType.MESH
f32 = jnp.float32
bf16 = jnp.bfloat16
LANES = 128
highest = lax.Precision.HIGHEST


def up(value, unit):
    return -(-value // unit) * unit


def dot(a, b, on_a, on_b, precision=None):
    return lax.dot_general(
        a, b, (((on_a,), (on_b,)), ((), ())), preferred_element_type=f32, precision=precision
    )


def halves(value):
    top = value.astype(bf16)
    return top, (value - top.astype(f32)).astype(bf16)


def cos_sin(steps, period):
    quarter = jnp.floor(steps * (4.0 / period) + 0.5)
    phi = (steps - quarter * (period / 4)) * (2.0 * math.pi / period)
    z = phi * phi
    s = phi * (1 + z * (-1 / 6 + z * (1 / 120 + z * (-1 / 5040 + z * (1 / 362880)))))
    c = 1 + z * (-1 / 2 + z * (1 / 24 + z * (-1 / 720 + z * (1 / 40320 + z * (-1 / 3628800)))))
    turn = quarter - 4 * jnp.floor(quarter * 0.25)
    odd = (turn == 1) | (turn == 3)
    cosine = jnp.where(odd, s, c)
    sine = jnp.where(odd, c, s)
    cosine = jnp.where((turn == 1) | (turn == 2), -cosine, cosine)
    sine = jnp.where((turn == 2) | (turn == 3), -sine, sine)
    return cosine, sine


def kernel(
    n, slots, rows, lev, nn, lon,
    grad_hbm, remap_ref, modes_ref, balance_ref, leg_hbm, ctrl_hbm, step_ref, owner_ref,
    upd_ref, inc_ref,
    grad, gf, gext, gres, leg, lhl, ctrl, mnat, wave,
    send1, recv1, send2, recv2, xt, rt, xa, zc, va, ht, acc, mix, cbuf, crecv, dbuf, drecv, vbuf, ubuf,
    in_sem, send_sem, recv_sem, self_sem, cs_sem, cr_sem, ds_sem, dr_sem,
):
    me = lax.axis_index("lat")
    var = lax.axis_index("var")
    full = rows * lev // LANES
    rest = rows * lev - full * LANES
    room = up(rest, 8)
    tiles = slots * full + 1
    pad = send1.shape[1] // n
    wide = slots * n
    columns = nn // LANES

    barrier = pltpu.get_barrier_semaphore()

    @pl.loop(1, n)
    def _(k):
        pl.semaphore_signal(
            barrier, inc=1, device_id=(var, lax.rem(me + k, n)), device_id_type=MESH
        )

    pl.semaphore_signal(barrier, inc=1, device_id=(1 - var, me), device_id_type=MESH)

    grad_in = pltpu.make_async_copy(grad_hbm, grad, in_sem.at[0])
    grad_in.start()
    leg_in = [
        pltpu.make_async_copy(leg_hbm.at[:, :, pl.ds(LANES * j, LANES)], leg.at[j], in_sem.at[1 + j])
        for j in range(columns)
    ]
    for copy in leg_in:
        copy.start()
    ctrl_in = pltpu.make_async_copy(ctrl_hbm, ctrl, in_sem.at[1 + columns])
    ctrl_in.start()

    mnat[...] = jnp.broadcast_to(owner_ref[...].astype(f32), (LANES, slots * n)).T
    chunk = min(32, n)
    factor = math.sqrt(2.0 / lon)

    for s in range(slots):

        @pl.loop(0, n // chunk)
        def _(at, s=s):
            m = mnat[pl.ds(at * chunk * slots + s, chunk, stride=slots), :]
            lane = lax.broadcasted_iota(jnp.int32, (chunk, LANES), 1).astype(f32)
            turn_c, turn_s = cos_sin(m * LANES, lon)
            c, d = cos_sin(m * lane, lon)
            c = c * factor
            d = d * factor
            place = pl.ds(pl.multiple_of(s * n + at * chunk, 8), chunk)
            for j in range(lon // LANES):
                here = pl.ds(j * LANES, LANES)
                wave[0, 0, place, here], wave[0, 1, place, here] = halves(c)
                wave[1, 0, place, here], wave[1, 1, place, here] = halves(d)
                c, d = c * turn_c - d * turn_s, d * turn_c + c * turn_s

    grad_in.wait()
    for r in range(rows):
        gf[r * lev : (r + 1) * lev, :] = grad[r].astype(f32)
    for t in range(full):
        gext[t] = gf[t * LANES : (t + 1) * LANES, :].astype(bf16)
    for s in range(slots):
        gres[...] = jnp.zeros_like(gres)
        gres[s * room : s * room + rest, :] = gf[full * LANES : full * LANES + rest, :]
        gext[full + s] = gres[...].astype(bf16)

    pl.semaphore_wait(barrier, n)

    def message(device):
        return pl.ds(pl.multiple_of(device * pad, 8), tiles)

    def exchange(send, recv, part, way):
        @pl.loop(1, n)
        def _(k):
            to = lax.rem(me + k, n)
            pltpu.make_async_remote_copy(
                send.at[part, message(to)],
                recv.at[part, message(me)],
                send_sem.at[way, part],
                recv_sem.at[way, part],
                device_id=(var, to),
                device_id_type=MESH,
            ).start()

        pltpu.make_async_copy(
            send.at[part, message(me)],
            recv.at[part, message(me)],
            self_sem.at[way, part],
        ).start()

    def arrived(send, recv, part, way):
        pltpu.make_async_copy(
            send.at[part, message(me)],
            recv.at[part, message(me)],
            self_sem.at[way, part],
        ).wait()
        span = pl.ds(0, (n - 1) * tiles)
        pltpu.make_async_copy(
            recv.at[part, span],
            recv.at[part, span],
            recv_sem.at[way, part],
        ).wait()

    def sent(send, part, way):
        span = pl.ds(0, (n - 1) * tiles)
        pltpu.make_async_copy(
            send.at[part, span],
            send.at[part, span],
            send_sem.at[way, part],
        ).wait()

    def strip(buffer, part, q):
        return buffer.at[part, pl.ds(q, n, stride=pad), :]

    for part in range(2):
        left = None
        for s in range(slots):
            table = wave[part, :, s * n : (s + 1) * n, :].reshape(2 * n, lon)
            both = dot(table, gext[:full].reshape(full * LANES, lon), 1, 1)
            coef = both[:n] + both[n:]
            for t in range(full):
                strip(send1, part, s * full + t)[...] = coef[:, t * LANES : (t + 1) * LANES]
            both = dot(table, gext[full + s], 1, 1)
            term = both[:n] + both[n:]
            left = term if left is None else left + term
        strip(send1, part, tiles - 1)[...] = left
        exchange(send1, recv1, part, 0)

    for copy in leg_in:
        copy.wait()
    for s in range(slots):
        for r in range(rows):
            for j in range(columns):
                piece = leg[j, s, pl.ds(r, n, stride=rows), :]
                here = (slice(r * n, (r + 1) * n), slice(j * LANES, (j + 1) * LANES))
                lhl[(0, s) + here], lhl[(1, s) + here] = halves(piece)

    remap = remap_ref[...]
    modes = modes_ref[...]
    balance = balance_ref[...]
    mix[0, :lev, :lev] = dot(remap, modes, 1, 0, highest)
    mix[1, :lev, :lev] = dot(balance, modes, 1, 0, highest)
    mix[2, :lev, :lev] = dot(remap, balance, 1, 0, highest)
    rt[...] = jnp.zeros_like(rt)
    ctrl_in.wait()
    step = step_ref[0]

    def legendre_adjoint(part):
        rest_t = strip(recv1, part, tiles - 1)[...].T

        for s in range(slots):
            for t in range(full):
                xt[t * LANES : (t + 1) * LANES, :] = strip(recv1, part, s * full + t)[...].T
            xt[full * LANES : full * LANES + rest, :] = rest_t[s * room : s * room + rest]
            for r in range(rows):
                xa[0, :lev, r * n : (r + 1) * n], xa[1, :lev, r * n : (r + 1) * n] = halves(
                    xt[r * lev : (r + 1) * lev, :]
                )
            z = dot(xa[0, :lev], lhl[0, s], 1, 0)
            z = z + dot(xa[1, :lev], lhl[0, s], 1, 0)
            z = z + dot(xa[0, :lev], lhl[1, s], 1, 0)
            zc[part, :lev, s * nn : (s + 1) * nn] = z
        z = zc[part, :lev]

        @pl.when(var == 1)
        def _():
            cbuf[part, :lev] = dot(remap, z, 0, 0, highest)
            to_partner(cbuf, crecv, part, cs_sem, cr_sem).start()

    def to_partner(source, target, part, one, other):
        return pltpu.make_async_remote_copy(
            source.at[part],
            target.at[part],
            one.at[part],
            other.at[part],
            device_id=(1 - var, me),
            device_id_type=MESH,
        )

    def update(part):
        mode = dot(mix[0, :lev, :lev], zc[part, :lev], 0, 0, highest)
        ubuf[...] = mode

        @pl.when(var == 0)
        def _():
            to_partner(cbuf, crecv, part, cs_sem, cr_sem).wait_recv()
            ubuf[...] = ubuf[...] + dot(
                mix[1, :lev, :lev], crecv[part, :lev], 0, 0, highest
            )

        for s in range(slots):
            own = ctrl[s, part * lev : (part + 1) * lev, :]
            fresh = own - step * (own + ubuf[:, s * nn : (s + 1) * nn])
            upd_ref[s, part * lev : (part + 1) * lev, :] = fresh
            ubuf[:, s * nn : (s + 1) * nn] = fresh

        @pl.when(var == 0)
        def _():
            dbuf[part, :lev] = dot(modes, ubuf[...], 1, 0, highest)
            to_partner(dbuf, drecv, part, ds_sem, dr_sem).start()

        vbuf[part] = dot(mix[0, :lev, :lev], ubuf[...], 1, 0, highest)

    def legendre_forward(part):
        @pl.when(var == 1)
        def _():
            to_partner(dbuf, drecv, part, ds_sem, dr_sem).wait_recv()
            vbuf[part] = vbuf[part] + dot(mix[2, :lev, :lev], drecv[part, :lev], 1, 0, highest)

        for s in range(slots):
            va[0, :lev], va[1, :lev] = halves(vbuf[part, :, s * nn : (s + 1) * nn])
            y = dot(va[0, :lev], lhl[0, s], 1, 1)
            y = y + dot(va[1, :lev], lhl[0, s], 1, 1)
            y = y + dot(va[0, :lev], lhl[1, s], 1, 1)
            for r in range(rows):
                xt[r * lev : (r + 1) * lev, :] = y[:, r * n : (r + 1) * n]
            for t in range(full):
                strip(send2, part, s * full + t)[...] = xt[t * LANES : (t + 1) * LANES, :].T
            rt[s * room : s * room + rest, :] = xt[full * LANES : full * LANES + rest, :]
        strip(send2, part, tiles - 1)[...] = rt[...].T
        exchange(send2, recv2, part, 1)

    for part in range(2):
        arrived(send1, recv1, part, 0)
        legendre_adjoint(part)

        @pl.when(var == 0)
        def _(part=part):
            update(part)
            legendre_forward(part)

        @pl.when(var == 1)
        def _(part=part):
            update(part)
            if part == 1:
                legendre_forward(0)
                legendre_forward(1)

    for part in range(2):
        arrived(send2, recv2, part, 1)
        rest_t = strip(recv2, part, tiles - 1)[...].T
        for s in range(slots):
            here = slice(s * n, (s + 1) * n)
            for t in range(full):
                place = slice(t * LANES, (t + 1) * LANES)
                ht[0, place, here], ht[1, place, here] = halves(strip(recv2, part, s * full + t)[...].T)
            place = slice(full * LANES, full * LANES + rest)
            ht[0, place, here], ht[1, place, here] = halves(rest_t[s * room : s * room + rest])
        for j in range(lon // 512):
            here = slice(j * 512, (j + 1) * 512)
            top = wave[part, 0, :, here]
            sum_ = dot(ht[0], top, 1, 0)
            sum_ = sum_ + dot(ht[1], top, 1, 0)
            sum_ = sum_ + dot(ht[0], wave[part, 1, :, here], 1, 0)
            if part == 0:
                acc[:, here] = sum_
            else:
                acc[:, here] = acc[:, here] + sum_
    for r in range(rows):
        inc_ref[r] = acc[r * lev : (r + 1) * lev, :].astype(bf16)

    for part in range(2):
        sent(send1, part, 0)
        sent(send2, part, 1)

        @pl.when(var == 1)
        def _(part=part):
            to_partner(cbuf, crecv, part, cs_sem, cr_sem).wait_send()

        @pl.when(var == 0)
        def _(part=part):
            to_partner(dbuf, drecv, part, ds_sem, dr_sem).wait_send()


def local(n, grad_grid, remap, modes, balance, legendre, control, step_size, owner_slots):
    _, rows, lev, lon = grad_grid.shape
    slots, lats, nn = legendre.shape
    full = rows * lev // LANES
    rest = rows * lev - full * LANES
    assert slots * up(rest, 8) <= LANES and nn % LANES == 0 and lon % 512 == 0
    pad = up(slots * full + 1, 8)
    total = up(rows * lev, 16)
    columns = nn // LANES
    vmem = pl.BlockSpec(memory_space=pltpu.VMEM)
    anywhere = pl.BlockSpec(memory_space=pl.ANY)
    message = pltpu.VMEM((2, n * pad, LANES), f32)
    high = up(lev, 8)
    spectral = pltpu.VMEM((2, high, slots * nn), f32)
    dma = pltpu.SemaphoreType.DMA
    updated, increment = pl.pallas_call(
        functools.partial(kernel, n, slots, rows, lev, nn, lon),
        out_shape=(
            jax.ShapeDtypeStruct((slots, 2 * lev, nn), f32),
            jax.ShapeDtypeStruct((rows, lev, lon), bf16),
        ),
        in_specs=[
            anywhere, vmem, vmem, vmem, anywhere, anywhere,
            pl.BlockSpec(memory_space=pltpu.SMEM), vmem,
        ],
        out_specs=(vmem, vmem),
        scratch_shapes=[
            pltpu.VMEM((rows, lev, lon), bf16),
            pltpu.VMEM((up(rows * lev, 8), lon), f32),
            pltpu.VMEM((full + slots, LANES, lon), bf16),
            pltpu.VMEM((LANES, lon), f32),
            pltpu.VMEM((columns, slots, lats, LANES), f32),
            pltpu.VMEM((2, slots, lats, nn), bf16),
            pltpu.VMEM((slots, 2 * lev, nn), f32),
            pltpu.VMEM((slots * n, LANES), f32),
            pltpu.VMEM((2, 2, slots * n, lon), bf16),
            message, message, message, message,
            pltpu.VMEM((up(rows * lev, 8), n), f32),
            pltpu.VMEM((LANES, n), f32),
            pltpu.VMEM((2, up(lev, 16), rows * n), bf16),
            spectral,
            pltpu.VMEM((2, up(lev, 16), nn), bf16),
            pltpu.VMEM((2, rows * lev, slots * n), bf16),
            pltpu.VMEM((rows * lev, lon), f32),
            pltpu.VMEM((3, high, LANES), f32),
            spectral, spectral, spectral, spectral,
            pltpu.VMEM((2, lev, slots * nn), f32),
            pltpu.VMEM((lev, slots * nn), f32),
            dma((2 + columns,)), dma((2, 2)), dma((2, 2)), dma((2, 2)),
            dma((2,)), dma((2,)), dma((2,)), dma((2,)),
        ],
        compiler_params=pltpu.CompilerParams(
            collective_id=0, has_side_effects=True, vmem_limit_bytes=60 * 1024 * 1024
        ),
        name="step",
    )(
        grad_grid[0], remap[0], modes[0], balance, legendre, control[0],
        step_size, owner_slots.reshape(1, -1),
    )
    return updated[None], increment[None]


def solution(mesh):
    return jax.shard_map(
        functools.partial(local, mesh.shape["lat"]),
        mesh=mesh,
        in_specs=(
            P("var", "lat", None, None),
            P("var", None, None),
            P("var", None, None),
            P(),
            P("lat", None, None),
            P("var", "lat", None, None),
            P("var"),
            P(),
        ),
        out_specs=(P("var", "lat", None, None), P("var", "lat", None, None)),
        check_vma=False,
    )
```

```python
import functools
import math

import jax
import jax.numpy as jnp
from jax import lax
from jax.experimental import pallas as pl
from jax.experimental.pallas import tpu as pltpu
from jax.sharding import PartitionSpec as P

MESH = pl.DeviceIdType.MESH
f32 = jnp.float32
bf16 = jnp.bfloat16
LANES = 128
highest = lax.Precision.HIGHEST


def up(value, unit):
    return -(-value // unit) * unit


def dot(a, b, on_a, on_b, precision=None):
    return lax.dot_general(
        a, b, (((on_a,), (on_b,)), ((), ())), preferred_element_type=f32, precision=precision
    )


def halves(value):
    top = value.astype(bf16)
    return top, (value - top.astype(f32)).astype(bf16)


def cos_sin(steps, period):
    quarter = jnp.floor(steps * (4.0 / period) + 0.5)
    phi = (steps - quarter * (period / 4)) * (2.0 * math.pi / period)
    z = phi * phi
    s = phi * (1 + z * (-1 / 6 + z * (1 / 120 + z * (-1 / 5040 + z * (1 / 362880)))))
    c = 1 + z * (-1 / 2 + z * (1 / 24 + z * (-1 / 720 + z * (1 / 40320 + z * (-1 / 3628800)))))
    turn = quarter - 4 * jnp.floor(quarter * 0.25)
    odd = (turn == 1) | (turn == 3)
    cosine = jnp.where(odd, s, c)
    sine = jnp.where(odd, c, s)
    cosine = jnp.where((turn == 1) | (turn == 2), -cosine, cosine)
    sine = jnp.where((turn == 2) | (turn == 3), -sine, sine)
    return cosine, sine


def kernel(
    n, slots, rows, lev, nn, lon,
    grad_hbm, remap_ref, modes_ref, balance_ref, leg_hbm, ctrl_hbm, step_ref, owner_ref,
    upd_hbm, inc_ref,
    grad, gf, gext, gres, leg, lhl, ctrl, mnat, wave,
    send1a, send1b, recv1a, recv1b, send2a, send2b, recv2a, recv2b,
    xt, rt, xf, xa, va, hta, htb, htr, acc,
    oremap, omodes, steps, mats, amat, aop, cother, cs, ub, uown, uother, urecv,
    in_sem, send_sem, recv_sem, self_sem, swap_send, swap_recv, out_sem,
):
    me = lax.axis_index("lat")
    var = lax.axis_index("var")
    other = 1 - var
    full = rows * lev // LANES
    rest = rows * lev - full * LANES
    room = up(rest, 8)
    early = slots - 1
    pad = send1a.shape[1] // n
    high = up(lev, 8)
    columns = nn // LANES
    two = 2 * n

    barrier = pltpu.get_barrier_semaphore()

    def tell(plane, to):
        pl.semaphore_signal(barrier, inc=1, device_id=(plane, to), device_id_type=MESH)

    tell(other, me)

    @pl.loop(1, n)
    def _(k):
        to = lax.rem(me + k, n)
        tell(var, to)
        tell(other, to)

    grad_in = pltpu.make_async_copy(grad_hbm, grad, in_sem.at[0])
    grad_in.start()
    leg_in = [
        pltpu.make_async_copy(leg_hbm.at[:, :, pl.ds(LANES * j, LANES)], leg.at[j], in_sem.at[1 + j])
        for j in range(columns)
    ]
    ctrl_in = [
        pltpu.make_async_copy(
            ctrl_hbm.at[s, pl.ds(c * lev, lev), 0], ctrl.at[s, c], in_sem.at[1 + columns + 2 * s + c]
        )
        for s in range(slots)
        for c in range(2)
    ]
    for copy in ctrl_in + leg_in:
        copy.start()
    steps[var] = jnp.full(steps.shape[1:], step_ref[0], f32)

    owners = owner_ref[...].astype(f32).reshape(1, slots * n)
    mnat[...] = jnp.broadcast_to(owners, (LANES, slots * n)).T
    chunk = min(32, n)
    factor = math.sqrt(2.0 / lon)

    for s in range(slots):

        @pl.loop(0, n // chunk)
        def _(at, s=s):
            m = mnat[pl.ds(at * chunk * slots + s, chunk, stride=slots), :]
            lane = lax.broadcasted_iota(jnp.int32, (chunk, LANES), 1).astype(f32)
            turn_c, turn_s = cos_sin(m * LANES, lon)
            c, d = cos_sin(m * lane, lon)
            c = c * factor
            d = d * factor
            place = pl.ds(pl.multiple_of(s * two + at * chunk, 8), chunk)
            below = pl.ds(pl.multiple_of(s * two + n + at * chunk, 8), chunk)
            for j in range(lon // LANES):
                here = pl.ds(j * LANES, LANES)
                wave[0, place, here], wave[1, place, here] = halves(c)
                wave[0, below, here], wave[1, below, here] = halves(d)
                c, d = c * turn_c - d * turn_s, d * turn_c + c * turn_s

    grad_in.wait()
    for r in range(rows):
        gf[r * lev : (r + 1) * lev, :] = grad[r].astype(f32)
    for t in range(full):
        gext[t] = gf[t * LANES : (t + 1) * LANES, :].astype(bf16)
    for s in range(slots):
        gres[...] = jnp.zeros_like(gres)
        gres[s * room : s * room + rest, :] = gf[full * LANES : full * LANES + rest, :]
        gext[full + s] = gres[...].astype(bf16)

    def message(device, q):
        return pl.ds(pl.multiple_of(device * pad, 8), q)

    def strip(buffer, plane, q):
        return buffer.at[plane, pl.ds(q, n, stride=pad), :]

    def exchange(send, recv, q, stage):
        def to_device(plane, to, at):
            pltpu.make_async_remote_copy(
                send.at[plane, message(to, q)],
                recv.at[var, message(me, q)],
                send_sem.at[stage, at],
                recv_sem.at[stage, at],
                device_id=(plane, to),
                device_id_type=MESH,
            ).start()

        to_device(other, me, 1)

        @pl.loop(1, n)
        def _(k):
            to = lax.rem(me + k, n)
            to_device(var, to, 0)
            to_device(other, to, 1)

        own_block(send, recv, q, stage).start()

    def own_block(send, recv, q, stage):
        return pltpu.make_async_copy(
            send.at[var, message(me, q)], recv.at[var, message(me, q)], self_sem.at[stage]
        )

    def drain(buffer, q, sem):
        for at, count in enumerate((n - 1, n)):
            span = buffer.at[at, pl.ds(0, count * q)]
            pltpu.make_async_copy(span, span, sem.at[at]).wait()

    def arrived(send, recv, q, stage):
        own_block(send, recv, q, stage).wait()
        drain(recv, q, recv_sem.at[stage])

    def swap(source, target, at):
        return pltpu.make_async_remote_copy(
            source,
            target,
            swap_send.at[at],
            swap_recv.at[at],
            device_id=(other, me),
            device_id_type=MESH,
        )

    swaps = [
        swap(remap_ref, oremap, 0),
        swap(modes_ref, omodes, 1),
        swap(steps.at[var], steps.at[var], 2),
    ] + [swap(ctrl.at[s, other], cother.at[s], 3 + s) for s in range(slots)]
    returns = [swap(uother.at[s], urecv.at[s], 3 + slots + s) for s in range(slots)]

    def coefficients(s, columns_of):
        table = wave[:, s * two : (s + 1) * two, :].reshape(2 * two, lon)
        both = dot(table, columns_of, 1, 1)
        return both[:two] + both[two:]

    def to_strips(send, s, at):
        coef = coefficients(s, gext[:full].reshape(full * LANES, lon))
        for c in range(2):
            for t in range(full):
                strip(send, c, at + t)[...] = coef[
                    c * n : (c + 1) * n, t * LANES : (t + 1) * LANES
                ]

    for s in range(early):
        to_strips(send1a, s, s * full)
    left = coefficients(0, gext[full])
    for s in range(1, slots):
        left = left + coefficients(s, gext[full + s])
    for c in range(2):
        strip(send1a, c, early * full)[...] = left[c * n : (c + 1) * n]
    for copy in ctrl_in:
        copy.wait()
    pl.semaphore_wait(barrier, two - 1)
    exchange(send1a, recv1a, early * full + 1, 0)
    for copy in swaps:
        copy.start()
    to_strips(send1b, early, 0)
    exchange(send1b, recv1b, full, 1)

    for copy in leg_in:
        copy.wait()
    for s in range(slots):
        for r in range(rows):
            for j in range(columns):
                piece = leg[j, s, pl.ds(r, n, stride=rows), :]
                here = (slice(r * n, (r + 1) * n), slice(j * LANES, (j + 1) * LANES))
                lhl[(0, s) + here], lhl[(1, s) + here] = halves(piece)
    rt[...] = jnp.zeros_like(rt)
    xf[...] = jnp.zeros_like(xf)
    cs[...] = jnp.zeros_like(cs)
    amat[...] = jnp.zeros_like(amat)

    def level_operators():
        for copy in swaps[:3]:
            copy.wait_recv()
        mats[var, 0] = remap_ref[:, 0, :]
        mats[var, 1] = modes_ref[:, 0, :]
        mats[other, 0] = oremap[:, 0, :]
        mats[other, 1] = omodes[:, 0, :]
        both = balance_ref[...]
        first, second = slice(0, lev), slice(high, high + lev)
        amat[first, first] = dot(mats[0, 0], mats[0, 1], 1, 0, highest)
        amat[second, first] = dot(mats[1, 0], dot(both, mats[0, 1], 1, 0, highest), 1, 0, highest)
        amat[second, second] = dot(mats[1, 0], mats[1, 1], 1, 0, highest)
        aop[0], aop[1] = halves(amat[...].T)
        aop[2], aop[3] = halves(amat[...])

    def levels(at, value):
        top, low = halves(value)
        both = dot(aop[at : at + 2].reshape(4 * high, 2 * high), top, 1, 0)
        return both[: 2 * high] + both[2 * high :] + dot(aop[at], low, 1, 0)

    own_rows = pl.ds(pl.multiple_of(var * high, 8), lev)
    other_rows = pl.ds(pl.multiple_of(other * high, 8), lev)

    def spectral(s, recv, at, rest_t, send, to):
        for v in range(2):
            for t in range(full):
                xt[v, t * LANES : (t + 1) * LANES, :] = strip(recv, v, at + t)[...].T
            xt[v, full * LANES : full * LANES + rest, :] = rest_t[v][s * room : s * room + rest]
            for r in range(rows):
                xf[v * high : v * high + lev, r * n : (r + 1) * n] = xt[v, r * lev : (r + 1) * lev, :]
        xa[0], xa[1] = halves(xf[...])
        both = dot(xa[...].reshape(4 * high, rows * n), lhl[0, s], 1, 0)
        z = both[: 2 * high] + both[2 * high :] + dot(xa[0], lhl[1, s], 1, 0)
        mode = levels(0, z)
        swaps[3 + s].wait_recv()
        cs[own_rows] = ctrl[s, var]
        cs[other_rows] = cother[s]
        ub[: high] = jnp.broadcast_to(steps[0, :1, :1], (high, nn))
        ub[high:] = jnp.broadcast_to(steps[1, :1, :1], (high, nn))
        held = cs[...]
        fresh = held - ub[...] * (held + mode)
        ub[...] = fresh
        uown[s] = ub[own_rows]
        uother[s] = ub[other_rows]
        va[0], va[1] = halves(levels(2, fresh))
        both = dot(va[...].reshape(4 * high, nn), lhl[0, s], 1, 1)
        y = both[: 2 * high] + both[2 * high :] + dot(va[0], lhl[1, s], 1, 1)
        for v in range(2):
            for r in range(rows):
                xt[v, r * lev : (r + 1) * lev, :] = y[v * high : v * high + lev, r * n : (r + 1) * n]
            for t in range(full):
                strip(send, v, to + t)[...] = xt[v, t * LANES : (t + 1) * LANES, :].T
            rt[v, s * room : s * room + rest, :] = xt[v, full * LANES : full * LANES + rest, :]

    level_operators()
    arrived(send1a, recv1a, early * full + 1, 0)
    rest_t = [strip(recv1a, v, early * full)[...].T for v in range(2)]
    for s in range(early):
        spectral(s, recv1a, s * full, rest_t, send2a, s * full)
    exchange(send2a, recv2a, early * full, 2)
    arrived(send1b, recv1b, full, 1)
    spectral(early, recv1b, 0, rest_t, send2b, 0)
    for v in range(2):
        strip(send2b, v, full)[...] = rt[v].T
    exchange(send2b, recv2b, full + 1, 3)
    for copy in returns:
        copy.start()
    out = [
        pltpu.make_async_copy(
            uown.at[s], upd_hbm.at[s, pl.ds(var * lev, lev), 0], out_sem.at[s]
        )
        for s in range(slots)
    ] + [
        pltpu.make_async_copy(
            urecv.at[s], upd_hbm.at[s, pl.ds(other * lev, lev), 0], out_sem.at[slots + s]
        )
        for s in range(slots)
    ]
    for copy in out[:slots]:
        copy.start()

    def product(left, place):
        def on(here):
            top = wave[0, place, here]
            m = left.shape[1]
            both = dot(left[...].reshape(2 * m, left.shape[2]), top, 1, 0)
            return both[:m] + both[m:] + dot(left[0], wave[1, place, here], 1, 0)

        return on

    arrived(send2a, recv2a, early * full, 2)
    for s in range(early):
        for c in range(2):
            here = slice(s * two + c * n, s * two + (c + 1) * n)
            for t in range(full):
                place = slice(t * LANES, (t + 1) * LANES)
                hta[0, place, here], hta[1, place, here] = halves(strip(recv2a, c, s * full + t)[...].T)
    piece = 512
    whole = slice(0, full * LANES)
    for j in range(lon // piece):
        here = slice(j * piece, (j + 1) * piece)
        acc[whole, here] = product(hta, slice(0, early * two))(here)

    arrived(send2b, recv2b, full + 1, 3)
    for c in range(2):
        here = slice(c * n, (c + 1) * n)
        for t in range(full):
            place = slice(t * LANES, (t + 1) * LANES)
            htb[0, place, here], htb[1, place, here] = halves(strip(recv2b, c, t)[...].T)
        last = strip(recv2b, c, full)[...].T
        for s in range(slots):
            here = slice(s * two + c * n, s * two + (c + 1) * n)
            htr[0, :rest, here], htr[1, :rest, here] = halves(last[s * room : s * room + rest])
    for j in range(lon // piece):
        here = slice(j * piece, (j + 1) * piece)
        acc[whole, here] = acc[whole, here] + product(htb, slice(early * two, slots * two))(here)
        acc[full * LANES : full * LANES + rest, here] = product(htr, slice(0, slots * two))(here)[:rest]
    for r in range(rows):
        inc_ref[r] = acc[r * lev : (r + 1) * lev, :].astype(bf16)

    for s in range(slots):
        returns[s].wait_recv()
        out[slots + s].start()
    drain(send1a, early * full + 1, send_sem.at[0])
    drain(send1b, full, send_sem.at[1])
    drain(send2a, early * full, send_sem.at[2])
    drain(send2b, full + 1, send_sem.at[3])
    for copy in swaps + returns:
        copy.wait_send()
    for copy in out:
        copy.wait()


def local(n, grad_grid, remap, modes, balance, legendre, control, step_size, owner_slots):
    _, rows, lev, lon = grad_grid.shape
    slots, lats, nn = legendre.shape
    full = rows * lev // LANES
    rest = rows * lev - full * LANES
    assert slots * up(rest, 8) <= LANES and nn % LANES == 0 and lon % 512 == 0
    pad = up((slots - 1) * full + 1, 8)
    columns = nn // LANES
    vmem = pl.BlockSpec(memory_space=pltpu.VMEM)
    anywhere = pl.BlockSpec(memory_space=pl.ANY)
    message = pltpu.VMEM((2, n * pad, LANES), f32)
    high = up(lev, 8)
    pair = 2 * high
    units = pltpu.VMEM((slots, lev, nn), f32)
    square = pltpu.VMEM((lev, 1, lev), f32)
    dma = pltpu.SemaphoreType.DMA
    updated, increment = pl.pallas_call(
        functools.partial(kernel, n, slots, rows, lev, nn, lon),
        out_shape=(
            jax.ShapeDtypeStruct((slots, 2 * lev, 1, nn), f32),
            jax.ShapeDtypeStruct((rows, lev, lon), bf16),
        ),
        in_specs=[
            anywhere, vmem, vmem, vmem, anywhere, anywhere,
            pl.BlockSpec(memory_space=pltpu.SMEM), vmem,
        ],
        out_specs=(anywhere, vmem),
        scratch_shapes=[
            pltpu.VMEM((rows, lev, lon), bf16),
            pltpu.VMEM((up(rows * lev, 8), lon), f32),
            pltpu.VMEM((full + slots, LANES, lon), bf16),
            pltpu.VMEM((LANES, lon), f32),
            pltpu.VMEM((columns, slots, lats, LANES), f32),
            pltpu.VMEM((2, slots, lats, nn), bf16),
            pltpu.VMEM((slots, 2, lev, nn), f32),
            pltpu.VMEM((slots * n, LANES), f32),
            pltpu.VMEM((2, slots * 2 * n, lon), bf16),
            message, message, message, message, message, message, message, message,
            pltpu.VMEM((2, up(rows * lev, 8), n), f32),
            pltpu.VMEM((2, LANES, n), f32),
            pltpu.VMEM((pair, rows * n), f32),
            pltpu.VMEM((2, pair, rows * n), bf16),
            pltpu.VMEM((2, pair, nn), bf16),
            pltpu.VMEM((2, full * LANES, (slots - 1) * 2 * n), bf16),
            pltpu.VMEM((2, full * LANES, 2 * n), bf16),
            pltpu.VMEM((2, up(rest, 16), slots * 2 * n), bf16),
            pltpu.VMEM((up(rows * lev, 8), lon), f32),
            square, square,
            pltpu.VMEM((2, 8, LANES), f32),
            pltpu.VMEM((2, 2, lev, lev), f32),
            pltpu.VMEM((pair, pair), f32),
            pltpu.VMEM((4, pair, pair), bf16),
            units,
            pltpu.VMEM((pair, nn), f32),
            pltpu.VMEM((pair, nn), f32),
            units, units, units,
            dma((1 + columns + 2 * slots,)),
            dma((4, 2)), dma((4, 2)), dma((4,)),
            dma((3 + 2 * slots,)), dma((3 + 2 * slots,)), dma((2 * slots,)),
        ],
        compiler_params=pltpu.CompilerParams(
            collective_id=0, has_side_effects=True, vmem_limit_bytes=60 * 1024 * 1024
        ),
        name="step",
    )(
        grad_grid[0],
        jnp.transpose(remap, (1, 0, 2)),
        jnp.transpose(modes, (1, 0, 2)),
        balance,
        legendre,
        jnp.transpose(control, (1, 2, 0, 3)),
        step_size,
        owner_slots,
    )
    return jnp.transpose(updated, (2, 0, 1, 3)), increment[None]


def solution(mesh):
    return jax.shard_map(
        functools.partial(local, mesh.shape["lat"]),
        mesh=mesh,
        in_specs=(
            P("var", "lat", None, None),
            P("var", None, None),
            P("var", None, None),
            P(),
            P("lat", None, None),
            P("var", "lat", None, None),
            P("var"),
            P(),
        ),
        out_specs=(P("var", "lat", None, None), P("var", "lat", None, None)),
        check_vma=False,
    )
```

```python
import functools
import math

import jax
import jax.numpy as jnp
from jax import lax
from jax.experimental import pallas as pl
from jax.experimental.pallas import tpu as pltpu
from jax.sharding import PartitionSpec as P

MESH = pl.DeviceIdType.MESH
f32 = jnp.float32
bf16 = jnp.bfloat16
LANES = 128
highest = lax.Precision.HIGHEST


def up(value, unit):
    return -(-value // unit) * unit


def dot(a, b, on_a, on_b, precision=None):
    return lax.dot_general(
        a, b, (((on_a,), (on_b,)), ((), ())), preferred_element_type=f32, precision=precision
    )


def halves(value):
    top = value.astype(bf16)
    return top, (value - top.astype(f32)).astype(bf16)


def cos_sin(steps, period):
    quarter = jnp.floor(steps * (4.0 / period) + 0.5)
    phi = (steps - quarter * (period / 4)) * (2.0 * math.pi / period)
    z = phi * phi
    s = phi * (1 + z * (-1 / 6 + z * (1 / 120 + z * (-1 / 5040 + z * (1 / 362880)))))
    c = 1 + z * (-1 / 2 + z * (1 / 24 + z * (-1 / 720 + z * (1 / 40320 + z * (-1 / 3628800)))))
    turn = quarter - 4 * jnp.floor(quarter * 0.25)
    odd = (turn == 1) | (turn == 3)
    cosine = jnp.where(odd, s, c)
    sine = jnp.where(odd, c, s)
    cosine = jnp.where((turn == 1) | (turn == 2), -cosine, cosine)
    sine = jnp.where((turn == 2) | (turn == 3), -sine, sine)
    return cosine, sine


def kernel(
    n, slots, rows, lev, nn, lon,
    grad_hbm, remap_hbm, modes_hbm, balance_hbm, leg_hbm, ctrl_hbm, step_ref, owner_hbm,
    upd_hbm, inc_ref,
    grad, gf, gext, leg, lhl, ctrl, mnat, wave,
    send1a, send1b, recv1a, recv1b, send2a, send2b, recv2a, recv2b,
    xt, rt, xf, xa, va, hta, htb, htr, acc,
    oremap, omodes, steps, mats, amat, aop, cother, cs, ub, uown, uother, urecv,
    owner_ref, remap_ref, modes_ref, balance_ref,
    small_sem, in_sem, send_sem, recv_sem, self_sem, swap_send, swap_recv, out_sem,
):
    me = lax.axis_index("lat")
    var = lax.axis_index("var")
    other = 1 - var
    full = rows * lev // LANES
    rest = rows * lev - full * LANES
    room = up(rest, 8)
    early = slots - 1
    pad = send1a.shape[1] // n
    high = up(lev, 8)
    columns = nn // LANES
    two = 2 * n

    barrier = pltpu.get_barrier_semaphore()
    small_in = [
        pltpu.make_async_copy(source, target, small_sem.at[at])
        for at, (source, target) in enumerate(
            (
                (owner_hbm, owner_ref),
                (remap_hbm, remap_ref),
                (modes_hbm, modes_ref),
                (balance_hbm, balance_ref),
            )
        )
    ]

    def tell(plane, to):
        pl.semaphore_signal(barrier, inc=1, device_id=(plane, to), device_id_type=MESH)

    for copy in small_in:
        copy.start()

    def everywhere(act):
        group = 8 if n % 8 == 0 else 2
        outer = n // group

        @pl.loop(0, outer)
        def _(q):
            if outer == 16:
                y, x = q // 4, lax.rem(q, 4)
                y = lax.rem(2 + 3 * y + 3 * (y // 2) + 2 * (y // 3), 4)
                x = lax.rem(2 + 3 * x + 3 * (x // 2) + 2 * (x // 3), 4)
                row = me // group
                row = lax.rem(row // 4 + y, 4) * 4 + lax.rem(lax.rem(row, 4) + x, 4)
            else:
                row = lax.rem(me // group + outer - 1 - q, outer)
            inner = lax.rem(me, group)
            for z in (2, 1, 3, 0) if group == 8 else (0,):
                for core in (1, 0):
                    to = row * group
                    to += lax.rem(inner // 2 + z, group // 2) * 2 + lax.rem(inner + core, 2)
                    act(other, to, 1)
                    if z == 0 and core == 0:

                        @pl.when(q < outer - 1)
                        def _(to=to):
                            act(var, to, 0)
                    else:
                        act(var, to, 0)

    everywhere(lambda plane, to, at: tell(plane, to))

    grad_in = pltpu.make_async_copy(grad_hbm, grad, in_sem.at[0])
    grad_in.start()
    leg_in = [
        pltpu.make_async_copy(leg_hbm.at[:, :, pl.ds(LANES * j, LANES)], leg.at[j], in_sem.at[1 + j])
        for j in range(columns)
    ]
    ctrl_in = [
        pltpu.make_async_copy(
            ctrl_hbm.at[s, pl.ds(c * lev, lev), 0], ctrl.at[s, c], in_sem.at[1 + columns + 2 * s + c]
        )
        for s in range(slots)
        for c in range(2)
    ]
    for copy in ctrl_in + leg_in:
        copy.start()
    steps[var] = jnp.full(steps.shape[1:], step_ref[0], f32)

    small_in[0].wait()
    owners = owner_ref[...].astype(f32).reshape(1, slots * n)
    mnat[...] = jnp.broadcast_to(owners, (LANES, slots * n)).T
    chunk = min(32, n)
    factor = math.sqrt(2.0 / lon)

    for s in range(slots):

        @pl.loop(0, n // chunk)
        def _(at, s=s):
            m = mnat[pl.ds(at * chunk * slots + s, chunk, stride=slots), :]
            lane = lax.broadcasted_iota(jnp.int32, (chunk, LANES), 1).astype(f32)
            turn_c, turn_s = cos_sin(m * LANES, lon)
            c, d = cos_sin(m * lane, lon)
            c = c * factor
            d = d * factor
            place = pl.ds(pl.multiple_of(s * two + at * chunk, 8), chunk)
            below = pl.ds(pl.multiple_of(s * two + n + at * chunk, 8), chunk)
            for j in range(lon // LANES):
                here = pl.ds(j * LANES, LANES)
                wave[0, place, here], wave[1, place, here] = halves(c)
                wave[0, below, here], wave[1, below, here] = halves(d)
                c, d = c * turn_c - d * turn_s, d * turn_c + c * turn_s

    grad_in.wait()
    for r in range(rows):
        gf[r * lev : (r + 1) * lev, :] = grad[r].astype(f32)
    gf[rows * lev :, :] = jnp.zeros((gf.shape[0] - rows * lev, lon), f32)
    for t in range(full + 1):
        gext[t] = gf[t * LANES : (t + 1) * LANES, :].astype(bf16)

    def message(device, q):
        return pl.ds(pl.multiple_of(device * pad, 8), q)

    def strip(buffer, plane, q):
        return buffer.at[plane, pl.ds(q, n, stride=pad), :]

    def exchange(send, recv, q, stage):
        def to_device(plane, to, at):
            pltpu.make_async_remote_copy(
                send.at[plane, message(to, q)],
                recv.at[var, message(me, q)],
                send_sem.at[stage, at],
                recv_sem.at[stage, at],
                device_id=(plane, to),
                device_id_type=MESH,
            ).start()

        own_block(send, recv, q, stage).start()
        everywhere(to_device)

    def own_block(send, recv, q, stage):
        return pltpu.make_async_copy(
            send.at[var, message(me, q)], recv.at[var, message(me, q)], self_sem.at[stage]
        )

    def drain(buffer, q, sem):
        for at, count in enumerate((n - 1, n)):
            span = buffer.at[at, pl.ds(0, count * q)]
            pltpu.make_async_copy(span, span, sem.at[at]).wait()

    def arrived(send, recv, q, stage):
        own_block(send, recv, q, stage).wait()
        drain(recv, q, recv_sem.at[stage])

    def swap(source, target, at):
        return pltpu.make_async_remote_copy(
            source,
            target,
            swap_send.at[at],
            swap_recv.at[at],
            device_id=(other, me),
            device_id_type=MESH,
        )

    swaps = [
        swap(remap_ref, oremap, 0),
        swap(modes_ref, omodes, 1),
        swap(steps.at[var], steps.at[var], 2),
    ] + [swap(ctrl.at[s, other], cother.at[s], 3 + s) for s in range(slots)]
    returns = [swap(uother.at[s], urecv.at[s], 3 + slots + s) for s in range(slots)]

    def coefficients(s, first, last):
        table = wave[:, s * two : (s + 1) * two, :].reshape(2 * two, lon)
        both = dot(table, gext[first:last].reshape((last - first) * LANES, lon), 1, 1)
        return both[:two] + both[two:]

    def to_strips(send, coef, at):
        for c in range(2):
            for t in range(full):
                strip(send, c, at + t)[...] = coef[
                    c * n : (c + 1) * n, t * LANES : (t + 1) * LANES
                ]

    left = coefficients(early, full, full + 1)
    left = pltpu.roll(left, early * room, 1)
    for s in range(early):
        coef = coefficients(s, 0, full + 1)
        to_strips(send1a, coef, s * full)
        term = coef[:, full * LANES :]
        left = left + (pltpu.roll(term, s * room, 1) if s else term)
    for c in range(2):
        strip(send1a, c, early * full)[...] = left[c * n : (c + 1) * n]
    for copy in ctrl_in + small_in[1:]:
        copy.wait()
    pl.semaphore_wait(barrier, two - 1)
    exchange(send1a, recv1a, early * full + 1, 0)
    for copy in swaps:
        copy.start()
    to_strips(send1b, coefficients(early, 0, full), 0)
    exchange(send1b, recv1b, full, 1)

    for copy in leg_in:
        copy.wait()
    for s in range(slots):
        for r in range(rows):
            for j in range(columns):
                piece = leg[j, s, pl.ds(r, n, stride=rows), :]
                here = (slice(r * n, (r + 1) * n), slice(j * LANES, (j + 1) * LANES))
                lhl[(0, s) + here], lhl[(1, s) + here] = halves(piece)
    rt[...] = jnp.zeros_like(rt)
    xf[...] = jnp.zeros_like(xf)
    cs[...] = jnp.zeros_like(cs)
    amat[...] = jnp.zeros_like(amat)

    def level_operators():
        for copy in swaps[:3]:
            copy.wait_recv()
        mats[var, 0] = remap_ref[:, 0, :]
        mats[var, 1] = modes_ref[:, 0, :]
        mats[other, 0] = oremap[:, 0, :]
        mats[other, 1] = omodes[:, 0, :]
        both = balance_ref[...]
        first, second = slice(0, lev), slice(high, high + lev)
        amat[first, first] = dot(mats[0, 0], mats[0, 1], 1, 0, highest)
        amat[second, first] = dot(mats[1, 0], dot(both, mats[0, 1], 1, 0, highest), 1, 0, highest)
        amat[second, second] = dot(mats[1, 0], mats[1, 1], 1, 0, highest)
        aop[0], aop[1] = halves(amat[...].T)
        aop[2], aop[3] = halves(amat[...])

    def levels(at, value):
        top, low = halves(value)
        both = dot(aop[at : at + 2].reshape(4 * high, 2 * high), top, 1, 0)
        return both[: 2 * high] + both[2 * high :] + dot(aop[at], low, 1, 0)

    own_rows = pl.ds(pl.multiple_of(var * high, 8), lev)
    other_rows = pl.ds(pl.multiple_of(other * high, 8), lev)

    def spectral(s, recv, at, rest_t, send, to):
        for v in range(2):
            for t in range(full):
                xt[v, t * LANES : (t + 1) * LANES, :] = strip(recv, v, at + t)[...].T
            xt[v, full * LANES : full * LANES + rest, :] = rest_t[v][s * room : s * room + rest]
            for r in range(rows):
                xf[v * high : v * high + lev, r * n : (r + 1) * n] = xt[v, r * lev : (r + 1) * lev, :]
        xa[0], xa[1] = halves(xf[...])
        both = dot(xa[...].reshape(4 * high, rows * n), lhl[0, s], 1, 0)
        z = both[: 2 * high] + both[2 * high :] + dot(xa[0], lhl[1, s], 1, 0)
        mode = levels(0, z)
        swaps[3 + s].wait_recv()
        cs[own_rows] = ctrl[s, var]
        cs[other_rows] = cother[s]
        ub[: high] = jnp.broadcast_to(steps[0, :1, :1], (high, nn))
        ub[high:] = jnp.broadcast_to(steps[1, :1, :1], (high, nn))
        held = cs[...]
        fresh = held - ub[...] * (held + mode)
        ub[...] = fresh
        uown[s] = ub[own_rows]
        uother[s] = ub[other_rows]
        va[0], va[1] = halves(levels(2, fresh))
        both = dot(va[...].reshape(4 * high, nn), lhl[0, s], 1, 1)
        y = both[: 2 * high] + both[2 * high :] + dot(va[0], lhl[1, s], 1, 1)
        for v in range(2):
            for r in range(rows):
                xt[v, r * lev : (r + 1) * lev, :] = y[v * high : v * high + lev, r * n : (r + 1) * n]
            for t in range(full):
                strip(send, v, to + t)[...] = xt[v, t * LANES : (t + 1) * LANES, :].T
            rt[v, s * room : s * room + rest, :] = xt[v, full * LANES : full * LANES + rest, :]

    level_operators()
    arrived(send1a, recv1a, early * full + 1, 0)
    rest_t = [strip(recv1a, v, early * full)[...].T for v in range(2)]
    for s in range(early):
        spectral(s, recv1a, s * full, rest_t, send2a, s * full)
    exchange(send2a, recv2a, early * full, 2)
    arrived(send1b, recv1b, full, 1)
    spectral(early, recv1b, 0, rest_t, send2b, 0)
    for v in range(2):
        strip(send2b, v, full)[...] = rt[v].T
    exchange(send2b, recv2b, full + 1, 3)
    for copy in returns:
        copy.start()
    out = [
        pltpu.make_async_copy(
            uown.at[s], upd_hbm.at[s, pl.ds(var * lev, lev), 0], out_sem.at[s]
        )
        for s in range(slots)
    ] + [
        pltpu.make_async_copy(
            urecv.at[s], upd_hbm.at[s, pl.ds(other * lev, lev), 0], out_sem.at[slots + s]
        )
        for s in range(slots)
    ]
    for copy in out[:slots]:
        copy.start()

    def product(left, place):
        def on(here):
            top = wave[0, place, here]
            m = left.shape[1]
            both = dot(left[...].reshape(2 * m, left.shape[2]), top, 1, 0)
            return both[:m] + both[m:] + dot(left[0], wave[1, place, here], 1, 0)

        return on

    arrived(send2a, recv2a, early * full, 2)
    for s in range(early):
        for c in range(2):
            here = slice(s * two + c * n, s * two + (c + 1) * n)
            for t in range(full):
                place = slice(t * LANES, (t + 1) * LANES)
                hta[0, place, here], hta[1, place, here] = halves(strip(recv2a, c, s * full + t)[...].T)
    piece = 512
    whole = slice(0, full * LANES)
    for j in range(lon // piece):
        here = slice(j * piece, (j + 1) * piece)
        acc[whole, here] = product(hta, slice(0, early * two))(here)

    arrived(send2b, recv2b, full + 1, 3)
    for c in range(2):
        here = slice(c * n, (c + 1) * n)
        for t in range(full):
            place = slice(t * LANES, (t + 1) * LANES)
            htb[0, place, here], htb[1, place, here] = halves(strip(recv2b, c, t)[...].T)
        last = strip(recv2b, c, full)[...].T
        for s in range(slots):
            here = slice(s * two + c * n, s * two + (c + 1) * n)
            htr[0, :rest, here], htr[1, :rest, here] = halves(last[s * room : s * room + rest])
    for j in range(lon // piece):
        here = slice(j * piece, (j + 1) * piece)
        acc[whole, here] = acc[whole, here] + product(htb, slice(early * two, slots * two))(here)
        acc[full * LANES : full * LANES + rest, here] = product(htr, slice(0, slots * two))(here)[:rest]
    for r in range(rows):
        inc_ref[r] = acc[r * lev : (r + 1) * lev, :].astype(bf16)

    for s in range(slots):
        returns[s].wait_recv()
        out[slots + s].start()
    drain(send1a, early * full + 1, send_sem.at[0])
    drain(send1b, full, send_sem.at[1])
    drain(send2a, early * full, send_sem.at[2])
    drain(send2b, full + 1, send_sem.at[3])
    for copy in swaps + returns:
        copy.wait_send()
    for copy in out:
        copy.wait()


def local(n, grad_grid, remap, modes, balance, legendre, control, step_size, owner_slots):
    _, rows, lev, lon = grad_grid.shape
    slots, lats, nn = legendre.shape
    full = rows * lev // LANES
    rest = rows * lev - full * LANES
    assert slots * up(rest, 8) <= LANES and nn % LANES == 0 and lon % 512 == 0
    pad = up((slots - 1) * full + 1, 8)
    columns = nn // LANES
    vmem = pl.BlockSpec(memory_space=pltpu.VMEM)
    anywhere = pl.BlockSpec(memory_space=pl.ANY)
    hbm = pl.BlockSpec(memory_space=pltpu.HBM)
    message = pltpu.VMEM((2, n * pad, LANES), f32)
    high = up(lev, 8)
    pair = 2 * high
    units = pltpu.VMEM((slots, lev, nn), f32)
    square = pltpu.VMEM((lev, 1, lev), f32)
    dma = pltpu.SemaphoreType.DMA
    outside = functools.partial(pltpu.with_memory_space_constraint, memory_space=pltpu.HBM)
    updated, increment = pl.pallas_call(
        functools.partial(kernel, n, slots, rows, lev, nn, lon),
        out_shape=(
            jax.ShapeDtypeStruct((slots, 2 * lev, 1, nn), f32),
            jax.ShapeDtypeStruct((rows, lev, lon), bf16),
        ),
        in_specs=[
            hbm, hbm, hbm, hbm, hbm, hbm,
            pl.BlockSpec(memory_space=pltpu.SMEM), hbm,
        ],
        out_specs=(anywhere, vmem),
        scratch_shapes=[
            pltpu.VMEM((rows, lev, lon), bf16),
            pltpu.VMEM(((full + 1) * LANES, lon), f32),
            pltpu.VMEM((full + 1, LANES, lon), bf16),
            pltpu.VMEM((columns, slots, lats, LANES), f32),
            pltpu.VMEM((2, slots, lats, nn), bf16),
            pltpu.VMEM((slots, 2, lev, nn), f32),
            pltpu.VMEM((slots * n, LANES), f32),
            pltpu.VMEM((2, slots * 2 * n, lon), bf16),
            message, message, message, message, message, message, message, message,
            pltpu.VMEM((2, up(rows * lev, 8), n), f32),
            pltpu.VMEM((2, LANES, n), f32),
            pltpu.VMEM((pair, rows * n), f32),
            pltpu.VMEM((2, pair, rows * n), bf16),
            pltpu.VMEM((2, pair, nn), bf16),
            pltpu.VMEM((2, full * LANES, (slots - 1) * 2 * n), bf16),
            pltpu.VMEM((2, full * LANES, 2 * n), bf16),
            pltpu.VMEM((2, up(rest, 16), slots * 2 * n), bf16),
            pltpu.VMEM((up(rows * lev, 8), lon), f32),
            square, square,
            pltpu.VMEM((2, 8, LANES), f32),
            pltpu.VMEM((2, 2, lev, lev), f32),
            pltpu.VMEM((pair, pair), f32),
            pltpu.VMEM((4, pair, pair), bf16),
            units,
            pltpu.VMEM((pair, nn), f32),
            pltpu.VMEM((pair, nn), f32),
            units, units, units,
            pltpu.VMEM(owner_slots.shape, jnp.int32),
            square, square, pltpu.VMEM((lev, lev), f32),
            dma((4,)),
            dma((1 + columns + 2 * slots,)),
            dma((4, 2)), dma((4, 2)), dma((4,)),
            dma((3 + 2 * slots,)), dma((3 + 2 * slots,)), dma((2 * slots,)),
        ],
        compiler_params=pltpu.CompilerParams(
            collective_id=0, has_side_effects=True, vmem_limit_bytes=48 * 1024 * 1024
        ),
        name="step",
    )(
        outside(grad_grid[0]),
        outside(jnp.transpose(remap, (1, 0, 2))),
        outside(jnp.transpose(modes, (1, 0, 2))),
        outside(balance),
        outside(legendre),
        outside(jnp.transpose(control, (1, 2, 0, 3))),
        step_size,
        outside(owner_slots),
    )
    return jnp.transpose(updated, (2, 0, 1, 3)), increment[None]


def solution(mesh):
    return jax.shard_map(
        functools.partial(local, mesh.shape["lat"]),
        mesh=mesh,
        in_specs=(
            P("var", "lat", None, None),
            P("var", None, None),
            P("var", None, None),
            P(),
            P("lat", None, None),
            P("var", "lat", None, None),
            P("var"),
            P(),
        ),
        out_specs=(P("var", "lat", None, None), P("var", "lat", None, None)),
        check_vma=False,
    )
```

```python
import functools
import math

import jax
import jax.numpy as jnp
from jax import lax
from jax.experimental import pallas as pl
from jax.experimental.pallas import tpu as pltpu
from jax.sharding import PartitionSpec as P

MESH = pl.DeviceIdType.MESH
f32 = jnp.float32
bf16 = jnp.bfloat16
LANES = 128
highest = lax.Precision.HIGHEST


def up(value, unit):
    return -(-value // unit) * unit


def dot(a, b, on_a, on_b, precision=None):
    return lax.dot_general(
        a, b, (((on_a,), (on_b,)), ((), ())), preferred_element_type=f32, precision=precision
    )


def halves(value):
    top = value.astype(bf16)
    return top, (value - top.astype(f32)).astype(bf16)


def cos_sin(steps, period):
    quarter = jnp.floor(steps * (4.0 / period) + 0.5)
    phi = (steps - quarter * (period / 4)) * (2.0 * math.pi / period)
    z = phi * phi
    s = phi * (1 + z * (-1 / 6 + z * (1 / 120 + z * (-1 / 5040 + z * (1 / 362880)))))
    c = 1 + z * (-1 / 2 + z * (1 / 24 + z * (-1 / 720 + z * (1 / 40320 + z * (-1 / 3628800)))))
    turn = quarter - 4 * jnp.floor(quarter * 0.25)
    odd = (turn == 1) | (turn == 3)
    cosine = jnp.where(odd, s, c)
    sine = jnp.where(odd, c, s)
    cosine = jnp.where((turn == 1) | (turn == 2), -cosine, cosine)
    sine = jnp.where((turn == 2) | (turn == 3), -sine, sine)
    return cosine, sine


def kernel(
    n, slots, rows, lev, nn, lon,
    grad_hbm, remap_hbm, modes_hbm, balance_hbm, leg_hbm, ctrl_hbm, step_ref, owner_hbm,
    uown, urecv, inc_ref,
    grad, gf, gext, leg, lhl, ctrl, mnat, wave,
    send1a, send1b, recv1a, recv1b, send2a, send2b, recv2a, recv2b,
    xt, rt, xf, xa, va, hta, htb, htr, acc,
    oremap, omodes, steps, mats, amat, aop, cother, cs, ub, uother,
    owner_ref, remap_ref, modes_ref, balance_ref,
    small_sem, in_sem, send_sem, recv_sem, self_sem, swap_send, swap_recv,
):
    me = lax.axis_index("lat")
    var = lax.axis_index("var")
    other = 1 - var
    full = rows * lev // LANES
    rest = rows * lev - full * LANES
    room = up(rest, 8)
    early = slots - 1
    pad = send1a.shape[1] // n
    high = up(lev, 8)
    columns = nn // LANES
    two = 2 * n

    barrier = pltpu.get_barrier_semaphore()
    small_in = [
        pltpu.make_async_copy(source, target, small_sem.at[at])
        for at, (source, target) in enumerate(
            (
                (owner_hbm, owner_ref),
                (remap_hbm, remap_ref),
                (modes_hbm, modes_ref),
                (balance_hbm, balance_ref),
            )
        )
    ]

    def tell(plane, to):
        pl.semaphore_signal(barrier, inc=1, device_id=(plane, to), device_id_type=MESH)

    for copy in small_in:
        copy.start()

    group = 8 if n % 8 == 0 else 2
    outer = n // group
    blocks = 4 if outer == 16 else 1
    width = n // blocks

    def far_first(digit):
        return (2 + 3 * digit + 3 * (digit // 2) + 2 * (digit // 3)) % 4

    def everywhere(act, first=0, last=outer, skip=None):
        @pl.loop(first, last)
        def _(q):
            if outer == 16:
                y, x = q // 4, lax.rem(q, 4)
                y = lax.rem(2 + 3 * y + 3 * (y // 2) + 2 * (y // 3), 4)
                x = lax.rem(2 + 3 * x + 3 * (x // 2) + 2 * (x // 3), 4)
                row = me // group
                row = lax.rem(row // 4 + y, 4) * 4 + lax.rem(lax.rem(row, 4) + x, 4)
            else:
                row = lax.rem(me // group + outer - 1 - q, outer)
            inner = lax.rem(me, group)
            for z in (2, 1, 3, 0) if group == 8 else (0,):
                for core in (1, 0):
                    to = row * group
                    to += lax.rem(inner // 2 + z, group // 2) * 2 + lax.rem(inner + core, 2)
                    here = z == 0 and core == 0
                    if skip is not None:
                        if here:

                            @pl.when(jnp.logical_not(skip) | (q < outer - 1))
                            def _(to=to):
                                act(to)
                        else:
                            act(to)
                        continue
                    act(other, to, 1)
                    if here:

                        @pl.when(q < outer - 1)
                        def _(to=to):
                            act(var, to, 0)
                    else:
                        act(var, to, 0)

    hub = lax.rem(var + me, 2) == 0

    @pl.when(hub)
    def _():
        tell(other, me)

    everywhere(lambda to: tell(lax.rem(to, 2), to), skip=hub)

    grad_in = pltpu.make_async_copy(grad_hbm, grad, in_sem.at[0])
    grad_in.start()
    leg_in = [
        pltpu.make_async_copy(leg_hbm.at[:, :, pl.ds(LANES * j, LANES)], leg.at[j], in_sem.at[1 + j])
        for j in range(columns)
    ]
    ctrl_in = [
        pltpu.make_async_copy(
            ctrl_hbm.at[s, pl.ds(c * lev, lev), 0], ctrl.at[s, c], in_sem.at[1 + columns + 2 * s + c]
        )
        for s in range(slots)
        for c in range(2)
    ]
    for copy in ctrl_in + leg_in:
        copy.start()
    steps[var] = jnp.full(steps.shape[1:], step_ref[0], f32)

    small_in[0].wait()
    owners = owner_ref[...].astype(f32).reshape(1, slots * n)
    mnat[...] = jnp.broadcast_to(owners, (LANES, slots * n)).T
    chunk = min(32, n)
    factor = math.sqrt(2.0 / lon)

    for s in range(slots):

        @pl.loop(0, n // chunk)
        def _(at, s=s):
            m = mnat[pl.ds(at * chunk * slots + s, chunk, stride=slots), :]
            lane = lax.broadcasted_iota(jnp.int32, (chunk, LANES), 1).astype(f32)
            turn_c, turn_s = cos_sin(m * LANES, lon)
            c, d = cos_sin(m * lane, lon)
            c = c * factor
            d = d * factor
            place = pl.ds(pl.multiple_of(s * two + at * chunk, 8), chunk)
            below = pl.ds(pl.multiple_of(s * two + n + at * chunk, 8), chunk)
            for j in range(lon // LANES):
                here = pl.ds(j * LANES, LANES)
                wave[0, place, here], wave[1, place, here] = halves(c)
                wave[0, below, here], wave[1, below, here] = halves(d)
                c, d = c * turn_c - d * turn_s, d * turn_c + c * turn_s

    def swap(source, target, at):
        return pltpu.make_async_remote_copy(
            source,
            target,
            swap_send.at[at],
            swap_recv.at[at],
            device_id=(other, me),
            device_id_type=MESH,
        )

    swaps = [
        swap(remap_ref, oremap, 0),
        swap(modes_ref, omodes, 1),
        swap(steps.at[var], steps.at[var], 2),
    ] + [swap(ctrl.at[s, other], cother.at[s], 3 + s) for s in range(slots)]
    returns = [swap(uother.at[s], urecv.at[s], 3 + slots + s) for s in range(slots)]

    for copy in ctrl_in + small_in[1:]:
        copy.wait()

    @pl.when(jnp.logical_not(hub))
    def _():
        pl.semaphore_wait(barrier, 1)
        for copy in swaps:
            copy.start()

    grad_in.wait()
    for r in range(rows):
        gf[r * lev : (r + 1) * lev, :] = grad[r].astype(f32)
    gf[rows * lev :, :] = jnp.zeros((gf.shape[0] - rows * lev, lon), f32)
    for t in range(full + 1):
        gext[t] = gf[t * LANES : (t + 1) * LANES, :].astype(bf16)

    def message(device, q):
        return pl.ds(pl.multiple_of(device * pad, 8), q)

    def strip(buffer, plane, q):
        return buffer.at[plane, pl.ds(q, n, stride=pad), :]

    def exchange(send, recv, q, stage, blocks_done=None):
        def to_device(plane, to, at):
            pltpu.make_async_remote_copy(
                send.at[plane, message(to, q)],
                recv.at[var, message(me, q)],
                send_sem.at[stage, at],
                recv_sem.at[stage, at],
                device_id=(plane, to),
                device_id_type=MESH,
            ).start()

        if blocks_done is None:
            own_block(send, recv, q, stage).start()
            everywhere(to_device)
        else:
            everywhere(to_device, blocks_done * (outer // blocks), (blocks_done + 1) * (outer // blocks))
            if blocks_done == blocks - 1:
                own_block(send, recv, q, stage).start()

    def own_block(send, recv, q, stage):
        return pltpu.make_async_copy(
            send.at[var, message(me, q)], recv.at[var, message(me, q)], self_sem.at[stage]
        )

    def drain(buffer, q, sem):
        for at, count in enumerate((n - 1, n)):
            span = buffer.at[at, pl.ds(0, count * q)]
            pltpu.make_async_copy(span, span, sem.at[at]).wait()

    def arrived(send, recv, q, stage):
        own_block(send, recv, q, stage).wait()
        drain(recv, q, recv_sem.at[stage])

    def coefficients(s, first, last):
        table = wave[:, s * two : (s + 1) * two, :].reshape(2 * two, lon)
        both = dot(table, gext[first:last].reshape((last - first) * LANES, lon), 1, 1)
        return both[:two] + both[two:]

    def to_strips(send, coef, at):
        for c in range(2):
            for t in range(full):
                strip(send, c, at + t)[...] = coef[
                    c * n : (c + 1) * n, t * LANES : (t + 1) * LANES
                ]

    def block_table(s, start):
        return [
            wave[half, pl.ds(pl.multiple_of(s * two + c * n + start, 8), width), :]
            for half in range(2)
            for c in range(2)
        ]

    for block in range(blocks):
        start = 0
        if blocks == 4:
            start = lax.rem(me // width + far_first(block), blocks) * width
        tables = sum([block_table(s, start) for s in range(early)], [])
        main = dot(
            jnp.concatenate(tables, axis=0), gext[...].reshape((full + 1) * LANES, lon), 1, 1
        )
        last = dot(jnp.concatenate(block_table(early, start), axis=0), gext[full], 1, 1)
        for c in range(2):

            def both(product, at):
                at = (at + c) * width
                return product[at : at + width] + product[at + 2 * width : at + 3 * width]

            def place(q):
                return send1a.at[c, pl.ds(start * pad + q, width, stride=pad), :]

            left = pltpu.roll(both(last, 0), early * room, 1)
            for s in range(early):
                coef = both(main, 4 * s)
                for t in range(full):
                    place(s * full + t)[...] = coef[:, t * LANES : (t + 1) * LANES]
                term = coef[:, full * LANES :]
                left = left + (pltpu.roll(term, s * room, 1) if s else term)
            place(early * full)[...] = left
        if block == 0:

            @pl.when(hub)
            def _():
                pl.semaphore_wait(barrier, two - 1)
                tell(other, me)

            @pl.when(jnp.logical_not(hub))
            def _():
                pl.semaphore_wait(barrier, 1)

        exchange(send1a, recv1a, early * full + 1, 0, block)

    @pl.when(hub)
    def _():
        for copy in swaps:
            copy.start()

    to_strips(send1b, coefficients(early, 0, full), 0)
    exchange(send1b, recv1b, full, 1)

    for copy in leg_in:
        copy.wait()
    for s in range(slots):
        for r in range(rows):
            for j in range(columns):
                piece = leg[j, s, pl.ds(r, n, stride=rows), :]
                here = (slice(r * n, (r + 1) * n), slice(j * LANES, (j + 1) * LANES))
                lhl[(0, s) + here], lhl[(1, s) + here] = halves(piece)
    rt[...] = jnp.zeros_like(rt)
    xf[...] = jnp.zeros_like(xf)
    cs[...] = jnp.zeros_like(cs)
    amat[...] = jnp.zeros_like(amat)

    def level_operators():
        for copy in swaps[:3]:
            copy.wait_recv()
        mats[var, 0] = remap_ref[:, 0, :]
        mats[var, 1] = modes_ref[:, 0, :]
        mats[other, 0] = oremap[:, 0, :]
        mats[other, 1] = omodes[:, 0, :]
        both = balance_ref[...]
        first, second = slice(0, lev), slice(high, high + lev)
        amat[first, first] = dot(mats[0, 0], mats[0, 1], 1, 0, highest)
        amat[second, first] = dot(mats[1, 0], dot(both, mats[0, 1], 1, 0, highest), 1, 0, highest)
        amat[second, second] = dot(mats[1, 0], mats[1, 1], 1, 0, highest)
        aop[0], aop[1] = halves(amat[...].T)
        aop[2], aop[3] = halves(amat[...])

    def levels(at, value):
        top, low = halves(value)
        both = dot(aop[at : at + 2].reshape(4 * high, 2 * high), top, 1, 0)
        return both[: 2 * high] + both[2 * high :] + dot(aop[at], low, 1, 0)

    own_rows = pl.ds(pl.multiple_of(var * high, 8), lev)
    other_rows = pl.ds(pl.multiple_of(other * high, 8), lev)

    def spectral(s, recv, at, rest_t, send, to):
        for v in range(2):
            for t in range(full):
                xt[v, t * LANES : (t + 1) * LANES, :] = strip(recv, v, at + t)[...].T
            xt[v, full * LANES : full * LANES + rest, :] = rest_t[v][s * room : s * room + rest]
            for r in range(rows):
                xf[v * high : v * high + lev, r * n : (r + 1) * n] = xt[v, r * lev : (r + 1) * lev, :]
        xa[0], xa[1] = halves(xf[...])
        both = dot(xa[...].reshape(4 * high, rows * n), lhl[0, s], 1, 0)
        z = both[: 2 * high] + both[2 * high :] + dot(xa[0], lhl[1, s], 1, 0)
        mode = levels(0, z)
        swaps[3 + s].wait_recv()
        cs[own_rows] = ctrl[s, var]
        cs[other_rows] = cother[s]
        ub[: high] = jnp.broadcast_to(steps[0, :1, :1], (high, nn))
        ub[high:] = jnp.broadcast_to(steps[1, :1, :1], (high, nn))
        held = cs[...]
        fresh = held - ub[...] * (held + mode)
        ub[...] = fresh
        uown[s] = ub[own_rows]
        uother[s] = ub[other_rows]
        va[0], va[1] = halves(levels(2, fresh))
        both = dot(va[...].reshape(4 * high, nn), lhl[0, s], 1, 1)
        y = both[: 2 * high] + both[2 * high :] + dot(va[0], lhl[1, s], 1, 1)
        for v in range(2):
            for r in range(rows):
                xt[v, r * lev : (r + 1) * lev, :] = y[v * high : v * high + lev, r * n : (r + 1) * n]
            for t in range(full):
                strip(send, v, to + t)[...] = xt[v, t * LANES : (t + 1) * LANES, :].T
            rt[v, s * room : s * room + rest, :] = xt[v, full * LANES : full * LANES + rest, :]

    level_operators()
    arrived(send1a, recv1a, early * full + 1, 0)
    rest_t = [strip(recv1a, v, early * full)[...].T for v in range(2)]
    for s in range(early):
        spectral(s, recv1a, s * full, rest_t, send2a, s * full)
    exchange(send2a, recv2a, early * full, 2)
    arrived(send1b, recv1b, full, 1)
    spectral(early, recv1b, 0, rest_t, send2b, 0)
    for v in range(2):
        strip(send2b, v, full)[...] = rt[v].T
    exchange(send2b, recv2b, full + 1, 3)
    for copy in returns:
        copy.start()

    def product(left, place):
        def on(here):
            top = wave[0, place, here]
            m = left.shape[1]
            both = dot(left[...].reshape(2 * m, left.shape[2]), top, 1, 0)
            return both[:m] + both[m:] + dot(left[0], wave[1, place, here], 1, 0)

        return on

    arrived(send2a, recv2a, early * full, 2)
    for s in range(early):
        for c in range(2):
            here = slice(s * two + c * n, s * two + (c + 1) * n)
            for t in range(full):
                place = slice(t * LANES, (t + 1) * LANES)
                hta[0, place, here], hta[1, place, here] = halves(strip(recv2a, c, s * full + t)[...].T)
    piece = 512
    whole = slice(0, full * LANES)
    for j in range(lon // piece):
        here = slice(j * piece, (j + 1) * piece)
        acc[whole, here] = product(hta, slice(0, early * two))(here)

    arrived(send2b, recv2b, full + 1, 3)
    for c in range(2):
        here = slice(c * n, (c + 1) * n)
        for t in range(full):
            place = slice(t * LANES, (t + 1) * LANES)
            htb[0, place, here], htb[1, place, here] = halves(strip(recv2b, c, t)[...].T)
        last = strip(recv2b, c, full)[...].T
        for s in range(slots):
            here = slice(s * two + c * n, s * two + (c + 1) * n)
            htr[0, :rest, here], htr[1, :rest, here] = halves(last[s * room : s * room + rest])
    for j in range(lon // piece):
        here = slice(j * piece, (j + 1) * piece)
        acc[whole, here] = acc[whole, here] + product(htb, slice(early * two, slots * two))(here)
        acc[full * LANES : full * LANES + rest, here] = product(htr, slice(0, slots * two))(here)[:rest]
    for r in range(rows):
        inc_ref[r] = acc[r * lev : (r + 1) * lev, :].astype(bf16)

    for s in range(slots):
        returns[s].wait_recv()
    drain(send1a, early * full + 1, send_sem.at[0])
    drain(send1b, full, send_sem.at[1])
    drain(send2a, early * full, send_sem.at[2])
    drain(send2b, full + 1, send_sem.at[3])
    for copy in swaps + returns:
        copy.wait_send()


def place_results(own, back, rounded, upd, inc, upd_sem, inc_sem):
    var = lax.axis_index("var")
    slots, lev, _ = own.shape
    copies = [
        pltpu.make_async_copy(rounded.at[r], inc.at[r], inc_sem.at[r]) for r in range(inc.shape[0])
    ]
    for s in range(slots):
        for at, (source, part) in enumerate(((own, var), (back, 1 - var))):
            target = upd.at[s, pl.ds(part * lev, lev), 0]
            copies.append(pltpu.make_async_copy(source.at[s], target, upd_sem.at[at, s]))
    for copy in copies:
        copy.start()
    for copy in copies:
        copy.wait()


def local(n, grad_grid, remap, modes, balance, legendre, control, step_size, owner_slots):
    _, rows, lev, lon = grad_grid.shape
    slots, lats, nn = legendre.shape
    full = rows * lev // LANES
    rest = rows * lev - full * LANES
    assert slots * up(rest, 8) <= LANES and nn % LANES == 0 and lon % 512 == 0
    pad = up((slots - 1) * full + 1, 8)
    columns = nn // LANES
    vmem = pl.BlockSpec(memory_space=pltpu.VMEM)
    anywhere = pl.BlockSpec(memory_space=pl.ANY)
    hbm = pl.BlockSpec(memory_space=pltpu.HBM)
    message = pltpu.VMEM((2, n * pad, LANES), f32)
    high = up(lev, 8)
    pair = 2 * high
    units = pltpu.VMEM((slots, lev, nn), f32)
    square = pltpu.VMEM((lev, 1, lev), f32)
    dma = pltpu.SemaphoreType.DMA
    outside = functools.partial(pltpu.with_memory_space_constraint, memory_space=pltpu.HBM)
    own, back, rounded = pl.pallas_call(
        functools.partial(kernel, n, slots, rows, lev, nn, lon),
        out_shape=(
            jax.ShapeDtypeStruct((slots, lev, nn), f32),
            jax.ShapeDtypeStruct((slots, lev, nn), f32),
            jax.ShapeDtypeStruct((rows, lev, lon), bf16),
        ),
        in_specs=[
            hbm, hbm, hbm, hbm, hbm, hbm,
            pl.BlockSpec(memory_space=pltpu.SMEM), hbm,
        ],
        out_specs=(vmem, vmem, vmem),
        scratch_shapes=[
            pltpu.VMEM((rows, lev, lon), bf16),
            pltpu.VMEM(((full + 1) * LANES, lon), f32),
            pltpu.VMEM((full + 1, LANES, lon), bf16),
            pltpu.VMEM((columns, slots, lats, LANES), f32),
            pltpu.VMEM((2, slots, lats, nn), bf16),
            pltpu.VMEM((slots, 2, lev, nn), f32),
            pltpu.VMEM((slots * n, LANES), f32),
            pltpu.VMEM((2, slots * 2 * n, lon), bf16),
            message, message, message, message, message, message, message, message,
            pltpu.VMEM((2, up(rows * lev, 8), n), f32),
            pltpu.VMEM((2, LANES, n), f32),
            pltpu.VMEM((pair, rows * n), f32),
            pltpu.VMEM((2, pair, rows * n), bf16),
            pltpu.VMEM((2, pair, nn), bf16),
            pltpu.VMEM((2, full * LANES, (slots - 1) * 2 * n), bf16),
            pltpu.VMEM((2, full * LANES, 2 * n), bf16),
            pltpu.VMEM((2, up(rest, 16), slots * 2 * n), bf16),
            pltpu.VMEM((up(rows * lev, 8), lon), f32),
            square, square,
            pltpu.VMEM((2, 8, LANES), f32),
            pltpu.VMEM((2, 2, lev, lev), f32),
            pltpu.VMEM((pair, pair), f32),
            pltpu.VMEM((4, pair, pair), bf16),
            units,
            pltpu.VMEM((pair, nn), f32),
            pltpu.VMEM((pair, nn), f32),
            units,
            pltpu.VMEM(owner_slots.shape, jnp.int32),
            square, square, pltpu.VMEM((lev, lev), f32),
            dma((4,)),
            dma((1 + columns + 2 * slots,)),
            dma((4, 2)), dma((4, 2)), dma((4,)),
            dma((3 + 2 * slots,)), dma((3 + 2 * slots,)),
        ],
        compiler_params=pltpu.CompilerParams(
            collective_id=0, has_side_effects=True, vmem_limit_bytes=48 * 1024 * 1024
        ),
        name="step",
    )(
        outside(grad_grid[0]),
        outside(jnp.transpose(remap, (1, 0, 2))),
        outside(jnp.transpose(modes, (1, 0, 2))),
        outside(balance),
        outside(legendre),
        outside(jnp.transpose(control, (1, 2, 0, 3))),
        step_size,
        outside(owner_slots),
    )
    updated, increment = pl.pallas_call(
        place_results,
        out_shape=(
            jax.ShapeDtypeStruct((slots, 2 * lev, 1, nn), f32),
            jax.ShapeDtypeStruct((rows, lev, lon), bf16),
        ),
        in_specs=[anywhere, anywhere, anywhere],
        out_specs=(hbm, hbm),
        scratch_shapes=[dma((2, slots)), dma((rows,))],
        compiler_params=pltpu.CompilerParams(vmem_limit_bytes=1024 * 1024),
        name="results",
    )(own, back, rounded)
    return jnp.transpose(updated, (2, 0, 1, 3)), increment[None]


def solution(mesh):
    return jax.shard_map(
        functools.partial(local, mesh.shape["lat"]),
        mesh=mesh,
        in_specs=(
            P("var", "lat", None, None),
            P("var", None, None),
            P("var", None, None),
            P(),
            P("lat", None, None),
            P("var", "lat", None, None),
            P("var"),
            P(),
        ),
        out_specs=(P("var", "lat", None, None), P("var", "lat", None, None)),
        check_vma=False,
    )
```
